128 devices in a mesh: lat: 16 (over z, y), lon: 8 (over x, core).
Axes of the slice: x: 4, y: 4, z: 4, core: 2. Of those that a mesh axis runs over, the one named last changes fastest.
Arguments:
- encoder_features: bfloat16 [512, 256, 128], P('lat', 'lon'), may hold values from -6 to 6
- noise: bfloat16 [512, 256, 128], P('lat', 'lon'), may hold values from -6 to 6
- patch_cols: int32 [16, 32], P('lat'), may hold values from 0 to 255, as said below
- timesteps: int32 [16, 32], P('lat'), may hold values from 0 to 31
- w_conv: bfloat16 [1152, 128], replicated, may hold values from -0.1875 to 0.1875
- w_down: bfloat16 [512, 256], replicated, may hold values from -0.25 to 0.25
- w_up: bfloat16 [256, 512], replicated, may hold values from -0.375 to 0.375
- w_out: bfloat16 [128, 128], replicated, may hold values from -0.5 to 0.5
Outputs:
- feature_grad: float32 [512, 256, 128], P('lat', 'lon')
- grad_conv: float32 [1152, 128], replicated
- grad_down: float32 [512, 256], replicated
- grad_up: float32 [256, 512], replicated
- grad_out: float32 [128, 128], replicated
- loss_value: float32 [], replicated
The draws below stay inside these ranges and needn't reach their ends.
Inputs may be any that keep to these rules, and one draw needn't show every extreme that they name: `patch_cols`: in each band at most 12 patches start in one device's block of 32 longitude cells, and exactly 12 start in one block.
All inputs are finite; a program needn't handle non-finite values.
Results may differ from the reference program's by a relative error of at most 0.009.
Values may be sent and summed in bfloat16 or wider, within the bound.
No kernel may reach another device: no remote copies, remote signals or barrier semaphores. Data moves between devices by JAX's collectives and lax.ppermute only.
A program may use at most 64 MiB of HBM per device.

```python
import math
import jax
import jax.numpy as jnp
from jax import lax

C = 128
PATCH = 32
NSTEPS = 32
CLON = 32
NLAT = 512
NLON = 256
NPB = 32
PMAX = 12
N_LAT = 16
N_LON = 8


def draw_patch_cols(key, part):
    key_busy = jax.random.fold_in(key, 11)
    key_offset = jax.random.fold_in(key, 12)
    busiest = jax.random.randint(key_busy, (N_LAT, 1), 0, N_LON)
    slots = jnp.arange(NPB, dtype=jnp.int32)[None, :]
    others = (busiest + 1 + (slots - PMAX) % (N_LON - 1)) % N_LON
    owners = jnp.where(slots < PMAX, busiest, others)
    offsets = jax.random.randint(key_offset, (N_LAT, NPB), 0, CLON)
    return (owners * CLON + offsets).astype(jnp.int32)


def touch_ends(result, stream_key, low, largest):
    longest = result.shape.index(max(result.shape))
    spots = []
    for shift in (0, 1):
        where = [jax.random.randint(jax.random.fold_in(stream_key, axis), (), 0, length) for axis, length in enumerate(result.shape)]
        where[longest] = (where[longest] + shift) % result.shape[longest]
        spots.append(tuple(where))
    return result.at[spots[0]].set(low).at[spots[1]].set(largest)


def level_of(rng, shape, cuts, smallest, high):
    def one(axis_at, parts):
        steps = jax.random.uniform(jax.random.fold_in(jax.random.fold_in(rng, 6), axis_at), (parts,), jnp.float32, smallest / len(cuts), high / len(cuts))
        return jnp.repeat(jnp.exp(steps), shape[axis_at] // parts).reshape((-1,) + (1,) * (len(shape) - axis_at - 1))

    gain = one(*cuts[0])
    for cut in cuts[1:]:
        gain = gain * one(*cut)
    return gain


def scatter_about(rng, shape, width, most, split=(), kind=jnp.bfloat16):
    array = width * jax.random.normal(rng, shape, jnp.float32)
    if split:
        array = array * level_of(rng, shape, split, -0.22, 0.18)
    return jnp.clip(array, -most, most).astype(kind)


def setup_inputs(seed: int = 0) -> dict:
    splits = jax.random.split(jax.random.key(seed), 9)
    return {
        "encoder_features": scatter_about(splits[0], (NLAT, NLON, C), 1.0, 6.0, ((0, 16), (1, 8))),
        "noise": scatter_about(splits[1], (NLAT, NLON, C), 1.0, 6.0, ((0, 16), (1, 8))),
        "patch_cols": draw_patch_cols(jax.random.fold_in(splits[8], 71), 0),
        "timesteps": touch_ends(jax.random.randint(splits[3], (N_LAT, NPB), 0, NSTEPS), jax.random.fold_in(splits[3], 1), 0, NSTEPS - 1).astype(jnp.int32),
        "w_conv": scatter_about(splits[4], (9 * C, C), (9 * C) ** -0.5, 0.1875),
        "w_down": scatter_about(splits[5], (4 * C, 2 * C), (4 * C) ** -0.5, 0.25),
        "w_up": scatter_about(splits[6], (2 * C, 4 * C), (2 * C) ** -0.5, 0.375),
        "w_out": scatter_about(splits[7], (C, C), C ** -0.5, 0.5),
    }


sigma_low = 0.02
sigma_high = 20.0

def sigma_of(levels):
    return sigma_low * jnp.exp(levels.astype(jnp.float32) / (NSTEPS - 1) * math.log(sigma_high / sigma_low))

def patch_loss(feat, noise_patch, sigma, w_conv, w_down, w_up, w_out):
    side = feat.shape[0]
    chans = feat.shape[2]
    scale_in = 1.0 / jnp.sqrt(1.0 + sigma * sigma)
    hidden = (scale_in * (feat + sigma * noise_patch.astype(jnp.float32))).astype(jnp.bfloat16)
    padded = jnp.pad(hidden, ((1, 1), (1, 1), (0, 0)))
    stacked = jnp.concatenate([padded[row_off:row_off + side, col_off:col_off + side] for row_off in range(3) for col_off in range(3)], axis=-1).reshape(side * side, 9 * chans)
    first = jax.nn.silu(jnp.dot(stacked, w_conv, preferred_element_type=jnp.float32)).astype(jnp.bfloat16)
    coarse_in = first.reshape(side // 2, 2, side // 2, 2, chans).transpose(0, 2, 1, 3, 4).reshape(side * side // 4, 4 * chans)
    coarse = jax.nn.silu(jnp.dot(coarse_in, w_down, preferred_element_type=jnp.float32)).astype(jnp.bfloat16)
    upward = jnp.dot(coarse, w_up, preferred_element_type=jnp.float32).reshape(side // 2, side // 2, 2, 2, chans).transpose(0, 2, 1, 3, 4).reshape(side * side, chans)
    merged = (first.astype(jnp.float32) + upward).astype(jnp.bfloat16)
    predicted = jnp.dot(merged, w_out, preferred_element_type=jnp.float32)
    error = predicted - noise_patch.reshape(side * side, chans).astype(jnp.float32)
    return jnp.sum(error * error) / (2.0 * chans)

def patch_grads(window_feat, window_noise, start, sigma, weights, live):
    side = window_feat.shape[0]
    feat = lax.dynamic_slice_in_dim(window_feat, start, side, 1).astype(jnp.float32)
    noise_patch = lax.dynamic_slice_in_dim(window_noise, start, side, 1)

    def local_loss(feat_in, conv_in, down_in, up_in, out_in):
        return patch_loss(feat_in, noise_patch, sigma, conv_in, down_in, up_in, out_in)
    value, pull = jax.vjp(local_loss, feat, *weights)
    return (value * live, pull(live))

def reference(encoder_features, noise, patch_cols, timesteps, w_conv, w_down, w_up, w_out):
    weights = (w_conv, w_down, w_up, w_out)
    side = PATCH
    chans = encoder_features.shape[2]

    def one_band(totals, band_index):
        feat_band = lax.dynamic_slice_in_dim(encoder_features, band_index * side, side, 0)
        noise_band = lax.dynamic_slice_in_dim(noise, band_index * side, side, 0)
        feat_ext = jnp.concatenate([feat_band, feat_band[:, :side]], axis=1)
        noise_ext = jnp.concatenate([noise_band, noise_band[:, :side]], axis=1)
        starts = lax.dynamic_index_in_dim(patch_cols, band_index, 0, keepdims=False)
        sigmas = sigma_of(lax.dynamic_index_in_dim(timesteps, band_index, 0, keepdims=False))

        def one_patch(inner, slot):
            grad_ext, sums = inner
            start = starts[slot]
            value, grads = patch_grads(feat_ext, noise_ext, start, sigmas[slot], weights, jnp.ones((), jnp.float32))
            current = lax.dynamic_slice_in_dim(grad_ext, start, side, 1)
            grad_ext = lax.dynamic_update_slice_in_dim(grad_ext, current + grads[0], start, 1)
            sums = tuple((total + part.astype(jnp.float32) for total, part in zip(sums[:4], grads[1:]))) + (sums[4] + value,)
            return ((grad_ext, sums), None)
        empty = jnp.zeros((side, NLON + side, chans), jnp.float32)
        (grad_ext, totals), unused = lax.scan(one_patch, (empty, totals), jnp.arange(NPB, dtype=jnp.int32))
        folded = grad_ext[:, :NLON].at[:, :side].add(grad_ext[:, NLON:])
        return (totals, folded)
    init = tuple((jnp.zeros(w.shape, jnp.float32) for w in weights)) + (jnp.zeros((), jnp.float32),)
    totals, band_grads = lax.scan(one_band, init, jnp.arange(N_LAT, dtype=jnp.int32))
    feature_grad = band_grads.reshape(NLAT, NLON, chans)
    loss_value = totals[4] / (N_LAT * NPB * side * side)
    return (feature_grad, totals[0], totals[1], totals[2], totals[3], loss_value)
```

```python
import math

import jax
import jax.numpy as jnp
from jax import lax
from jax.experimental import pallas as pl
from jax.experimental.pallas import tpu as pltpu
from jax.sharding import PartitionSpec as P

NSTEPS = 32
SIGMA_LOW = 0.02
SIGMA_HIGH = 20.0

SIDE = 32
HALF = SIDE // 2
GROUP = 8
M = GROUP * SIDE
MH = M // 2
OWN = 4
HALO = OWN + 2
CH = 128
INTERPRET = False

ROWS_CONV = 9 * CH
ROWS_DOWN = ROWS_CONV + 1024
ROWS_UP = ROWS_DOWN + 1024
ROWS_OUT = ROWS_UP + CH
ROWS_ALL = ROWS_OUT + 8

F32 = jnp.float32
BF16 = jnp.bfloat16


def mm(a, b, dims):
    return lax.dot_general(a, b, (dims, ((), ())), preferred_element_type=F32)


NN = ((1,), (0,))
NT = ((1,), (1,))
TN = ((0,), (0,))


def shift_cols(even, odd, place):
    down = pltpu.roll(odd.astype(F32), 1, 0)
    up = pltpu.roll(even.astype(F32), MH - 1, 0)
    down = jnp.where(place == 0, 0.0, down).astype(BF16)
    up = jnp.where(place == HALF - 1, 0.0, up).astype(BF16)
    return down, up


def band_kernel(
    cols_ref, rows_ref, scale_ref, sigma_ref, feat_ref, noise_ref,
    w_conv_ref, w_back_ref, w_down_ref, w_up_ref, w_out_ref,
    grad_ref, sums_ref,
    a_ref, ci_ref, d3_ref, du_ref, df_ref, fg_ref, gc_ref, gd_ref, loss_ref,
):
    step = pl.program_id(0)
    last = pl.num_programs(0) - 1
    nlon = feat_ref.shape[0]

    @pl.when(step == 0)
    def _():
        fg_ref[...] = jnp.zeros_like(fg_ref)
        gc_ref[...] = jnp.zeros_like(gc_ref)
        gd_ref[...] = jnp.zeros_like(gd_ref)
        loss_ref[...] = jnp.zeros_like(loss_ref)
        sums_ref[...] = jnp.zeros_like(sums_ref)

    scale = scale_ref[...]
    sigma = sigma_ref[...]
    pick = (lax.broadcasted_iota(jnp.int32, (M, nlon), 1) == cols_ref[...]).astype(F32).astype(BF16)
    feat = mm(pick, feat_ref[...], NN)
    noise = mm(pick, noise_ref[...], NN)
    hidden = (scale * (feat + sigma * noise)).astype(BF16)
    place_wide = lax.broadcasted_iota(jnp.int32, (MH, HALO * CH), 0) % HALF
    place = lax.broadcasted_iota(jnp.int32, (MH, CH), 0) % HALF

    even, odd = hidden[:MH], hidden[MH:]
    down, up = shift_cols(even, odd, place_wide)
    for r in range(OWN):
        for dr in range(3):
            src = slice((r + dr) * CH, (r + dr + 1) * CH)
            k = dr * 3 * CH
            a_ref[r * M : r * M + MH, k : k + CH] = down[:, src]
            a_ref[r * M + MH : (r + 1) * M, k : k + CH] = even[:, src]
            a_ref[r * M : (r + 1) * M, k + CH : k + 2 * CH] = hidden[:, src]
            a_ref[r * M : r * M + MH, k + 2 * CH : k + 3 * CH] = odd[:, src]
            a_ref[r * M + MH : (r + 1) * M, k + 2 * CH : k + 3 * CH] = up[:, src]

    pre = mm(a_ref[...], w_conv_ref[...], NN)
    gate = jax.nn.sigmoid(pre)
    first = (pre * gate).astype(BF16)
    slope = gate * (1.0 + pre * (1.0 - gate))

    for i in range(2):
        for k in range(4):
            start = (2 * i + k // 2) * M + (k % 2) * MH
            ci_ref[i * MH : (i + 1) * MH, k * CH : (k + 1) * CH] = first[start : start + MH]
    pre2 = mm(ci_ref[...], w_down_ref[...], NN)
    gate2 = jax.nn.sigmoid(pre2)
    coarse = (pre2 * gate2).astype(BF16)
    slope2 = gate2 * (1.0 + pre2 * (1.0 - gate2))
    upward = mm(coarse, w_up_ref[...], NN)

    spread = []
    for r in range(OWN):
        for q in range(2):
            k = (r % 2) * 2 + q
            spread.append(upward[(r // 2) * MH : (r // 2 + 1) * MH, k * CH : (k + 1) * CH])
    merged = (first.astype(F32) + jnp.concatenate(spread, axis=0)).astype(BF16)
    target = jnp.concatenate([noise[:, (r + 1) * CH : (r + 2) * CH] for r in range(OWN)], axis=0)
    error = mm(merged, w_out_ref[...], NN) - target
    loss_ref[...] += jnp.sum((error * error).reshape(-1, 8, CH), axis=0)
    d_pred = (error * (2.0 / (2.0 * CH))).astype(BF16)

    sums_ref[ROWS_UP:ROWS_OUT, :] += mm(merged, d_pred, TN)
    d_merged = mm(d_pred, w_out_ref[...], NT).astype(BF16)
    for i in range(2):
        for k in range(4):
            start = (2 * i + k // 2) * M + (k % 2) * MH
            du_ref[i * MH : (i + 1) * MH, k * CH : (k + 1) * CH] = d_merged[start : start + MH]
    d_up = du_ref[...]
    g_up = mm(coarse, d_up, TN)
    for k in range(4):
        sums_ref[ROWS_DOWN + k * 256 : ROWS_DOWN + (k + 1) * 256, :] += g_up[:, k * CH : (k + 1) * CH]
    d_coarse = mm(d_up, w_up_ref[...], NT).astype(BF16).astype(F32)
    d_pre2 = (d_coarse * slope2).astype(BF16)
    gd_ref[...] += mm(d_pre2, ci_ref[...], TN)
    d_ci = mm(d_pre2, w_down_ref[...], NT)
    spread = []
    for r in range(OWN):
        for q in range(2):
            k = (r % 2) * 2 + q
            spread.append(d_ci[(r // 2) * MH : (r // 2 + 1) * MH, k * CH : (k + 1) * CH])
    d_first = d_merged.astype(F32) + jnp.concatenate(spread, axis=0)
    d_pre = (d_first * slope).astype(BF16)
    gc_ref[...] += mm(d_pre, a_ref[...], TN)

    for r in range(OWN):
        even, odd = d_pre[r * M : r * M + MH], d_pre[r * M + MH : (r + 1) * M]
        down, up = shift_cols(even, odd, place)
        k = r * 3 * CH
        d3_ref[:MH, k : k + CH] = odd
        d3_ref[MH:, k : k + CH] = up
        d3_ref[:MH, k + CH : k + 2 * CH] = even
        d3_ref[MH:, k + CH : k + 2 * CH] = odd
        d3_ref[:MH, k + 2 * CH : k + 3 * CH] = down
        d3_ref[MH:, k + 2 * CH : k + 3 * CH] = even
    for r in range(HALO):
        lo, hi = max(0, r - 2), min(OWN - 1, r)
        wlo = (2 - (r - lo)) * 3 * CH
        width = (hi - lo + 1) * 3 * CH
        d_hidden = mm(
            d3_ref[:, lo * 3 * CH : lo * 3 * CH + width], w_back_ref[wlo : wlo + width, :], NN
        ).astype(BF16)
        df_ref[:, r * CH : (r + 1) * CH] = (scale * d_hidden.astype(F32)).astype(BF16)
    put = (lax.broadcasted_iota(jnp.int32, (nlon, M), 0) == rows_ref[0]).astype(F32).astype(BF16)
    fg_ref[...] += mm(put, df_ref[...], NN)

    @pl.when(step == last)
    def _():
        grad_ref[...] = fg_ref[...].astype(BF16)
        sums_ref[:ROWS_CONV, :] = gc_ref[...].T
        g_down = gd_ref[...].T
        sums_ref[ROWS_CONV : ROWS_CONV + 512, :] = g_down[:, :CH]
        sums_ref[ROWS_CONV + 512 : ROWS_DOWN, :] = g_down[:, CH:]
        sums_ref[ROWS_OUT:, :] = loss_ref[...]


def run_band(cols, scale, sigma, feat, noise, w_conv, w_back, w_down, w_up, w_out):
    steps = cols.shape[0] // M
    nlon = feat.shape[0]

    def whole(array):
        return pl.BlockSpec(array.shape, lambda g: (0,) * array.ndim)

    column = pl.BlockSpec((M, 1), lambda g: (g, 0))
    rows = cols.reshape(steps, 1, M)
    return pl.pallas_call(
        band_kernel,
        grid=(steps,),
        in_specs=[column, pl.BlockSpec((1, 1, M), lambda g: (g, 0, 0)), column, column]
        + [whole(x) for x in (feat, noise, w_conv, w_back, w_down, w_up, w_out)],
        out_specs=[
            pl.BlockSpec((nlon, HALO * CH), lambda g: (0, 0)),
            pl.BlockSpec((ROWS_ALL, CH), lambda g: (0, 0)),
        ],
        out_shape=[
            jax.ShapeDtypeStruct((nlon, HALO * CH), BF16),
            jax.ShapeDtypeStruct((ROWS_ALL, CH), F32),
        ],
        scratch_shapes=[
            pltpu.VMEM((OWN * M, 9 * CH), BF16),
            pltpu.VMEM((2 * MH, 4 * CH), BF16),
            pltpu.VMEM((M, OWN * 3 * CH), BF16),
            pltpu.VMEM((2 * MH, 4 * CH), BF16),
            pltpu.VMEM((M, HALO * CH), BF16),
            pltpu.VMEM((nlon, HALO * CH), F32),
            pltpu.VMEM((CH, 9 * CH), F32),
            pltpu.VMEM((2 * CH, 4 * CH), F32),
            pltpu.VMEM((8, CH), F32),
        ],
        interpret=INTERPRET,
    )(cols, rows, scale, sigma, feat, noise, w_conv, w_back, w_down, w_up, w_out)


def rows_for_devices(block, count):
    padded = jnp.pad(block, ((1, 1), (0, 0), (0, 0)))
    parts = jnp.stack([padded[OWN * d : OWN * d + HALO] for d in range(count)])
    return parts.transpose(0, 2, 1, 3).reshape(count, block.shape[1], HALO * CH)


def reduce_sums(sums):
    return lax.psum(sums, ("lat", "lon"))


def per_device(encoder_features, noise, patch_cols, timesteps, w_conv, w_down, w_up, w_out):
    count = lax.axis_size("lon")
    block_cols = encoder_features.shape[1]
    nlon = count * block_cols
    starts = patch_cols[0]
    patches = starts.shape[0]
    sigmas = SIGMA_LOW * jnp.exp(
        timesteps[0].astype(F32) / (NSTEPS - 1) * math.log(SIGMA_HIGH / SIGMA_LOW)
    )
    scales = 1.0 / jnp.sqrt(1.0 + sigmas * sigmas)

    sent = jnp.concatenate(
        [rows_for_devices(encoder_features, count), rows_for_devices(noise, count)], axis=1
    )
    got = lax.all_to_all(sent, "lon", 0, 0, tiled=True)
    feat_rows = got[:, :block_cols].reshape(nlon, HALO * CH)
    noise_rows = got[:, block_cols:].reshape(nlon, HALO * CH)

    groups = patches // GROUP
    offsets = jnp.arange(2)[None, :, None, None] + 2 * jnp.arange(HALF)[None, None, None, :]
    shape = (groups, 2, GROUP, HALF)

    def per_column(values):
        return jnp.broadcast_to(values.reshape(groups, 1, GROUP, 1), shape).reshape(-1, 1)

    cols = ((starts.reshape(groups, 1, GROUP, 1) + offsets) % nlon).astype(jnp.int32)
    w_back = w_conv.reshape(3, 3, CH, CH)[::-1].transpose(0, 1, 3, 2).reshape(9 * CH, CH)
    grad, sums = run_band(
        cols.reshape(-1, 1), per_column(scales), per_column(sigmas),
        feat_rows, noise_rows, w_conv, w_back, w_down, w_up, w_out,
    )

    back = lax.all_to_all(grad.reshape(count, block_cols, HALO * CH), "lon", 0, 0, tiled=True)
    back = back.reshape(count, block_cols, HALO, CH).transpose(0, 2, 1, 3).astype(F32)
    zero = jnp.zeros_like(back[:1, 0])
    above = jnp.concatenate([zero, back[:-1, HALO - 1]], axis=0)
    below = jnp.concatenate([back[1:, 0], zero], axis=0)
    own = back[:, 1 : OWN + 1]
    feature_grad = jnp.concatenate(
        [own[:, :1] + above[:, None], own[:, 1 : OWN - 1], own[:, OWN - 1 :] + below[:, None]],
        axis=1,
    ).reshape(encoder_features.shape)

    total = reduce_sums(sums)
    grad_conv = total[:ROWS_CONV]
    grad_down = jnp.concatenate(
        [total[ROWS_CONV : ROWS_CONV + 512], total[ROWS_CONV + 512 : ROWS_DOWN]], axis=1
    )
    grad_up = jnp.concatenate(
        [total[ROWS_DOWN + k * 256 : ROWS_DOWN + (k + 1) * 256] for k in range(4)], axis=1
    )
    grad_out = total[ROWS_UP:ROWS_OUT]
    cells = lax.axis_size("lat") * patches * SIDE * SIDE
    loss_value = jnp.sum(total[ROWS_OUT:]) / (2.0 * CH) / cells
    return (feature_grad, grad_conv, grad_down, grad_up, grad_out, loss_value)


def solution(mesh):
    placed = (P("lat", "lon", None), P("lat", "lon", None), P("lat", None), P("lat", None))
    return jax.shard_map(
        per_device,
        mesh=mesh,
        in_specs=placed + (P(), P(), P(), P()),
        out_specs=(P("lat", "lon", None), P(), P(), P(), P(), P()),
        check_vma=False,
    )
```
